128 devices in a mesh: segment: 4 (over y), seq: 32 (over x, z, core).
Axes of the slice: x: 4, y: 4, z: 4, core: 2. Of those that a mesh axis runs over, the one named last changes fastest.
Arguments:
- sr_tokens: bfloat16 [32768, 2048], P('seq'), may hold values from -6 to 6
- base_latent: bfloat16 [2048, 2048], P('seq'), may hold values from -6 to 6
- upsample_map: int32 [32768], P('seq'), may hold values from 0 to 2047, as said below
- norm_gain: float32 [2048], replicated, may hold values from 0.1 to 1.9
- w_qkv: bfloat16 [3, 2048, 2048], P(None, None, 'segment'), may hold values from -0.125 to 0.125
- qk_gain: float32 [2, 2048], P(None, 'segment'), may hold values from 0.42 to 10.4
- w_out: bfloat16 [2048, 2048], P('segment'), may hold values from -0.5 to 0.5
- block_lists: int32 [512, 8], replicated, may hold values from 0 to 511, as said below
- block_counts: int32 [512], replicated, may hold values from 1 to 8
Outputs:
- updated: bfloat16 [32768, 2048], P('seq', 'segment')
The draws below stay inside these ranges and needn't reach their ends.
Inputs may be any that keep to these rules, and one draw needn't show every extreme that they name: upsample_map[t] names a low-resolution token whose frame, index // 64, differs by at most one from t // 1024. block_lists[b, 0] = b, and the entries of one row are distinct.
All inputs are finite; a program needn't handle non-finite values.
Results may differ from the reference program's by a relative error of at most 0.012.
The reference program's roundings to bfloat16 on the way count: a program that leaves them out, or rounds other values in their place, can miss the bound.
Values may be sent and summed in bfloat16 or wider, within the bound.
No kernel may reach another device: no remote copies, remote signals or barrier semaphores. Data moves between devices by JAX's collectives and lax.ppermute only.
A program may use at most 128 MiB of HBM per device.

```python
import jax
import jax.numpy as jnp
from jax import lax

D = 2048
HEADS = 16
HD = 128
SIDE = 32
BASE_SIDE = 8
FRAME_TOK = 1024
BASE_FT = 64
SEQ_TOK = 32768
BASE_TOK = 2048
BLOCK = 64
WINDOW = 8
QBLOCKS = 512


def draw_upsample_map(key, part):
    tok_index = jnp.arange(SEQ_TOK, dtype=jnp.int32)
    frame_index = tok_index // FRAME_TOK
    spot_index = tok_index % FRAME_TOK
    row_index = spot_index // SIDE
    col_index = spot_index % SIDE
    key_frame, key_row, key_col = jax.random.split(key, 3)
    frame_total = SEQ_TOK // FRAME_TOK
    factor = SIDE // BASE_SIDE
    base_frame = jnp.clip(frame_index + jax.random.randint(key_frame, (SEQ_TOK,), -1, 2), 0, frame_total - 1)
    base_row = jnp.clip(row_index // factor + jax.random.randint(key_row, (SEQ_TOK,), -1, 2), 0, BASE_SIDE - 1)
    base_col = jnp.clip(col_index // factor + jax.random.randint(key_col, (SEQ_TOK,), -1, 2), 0, BASE_SIDE - 1)
    return (base_frame * BASE_FT + base_row * BASE_SIDE + base_col).astype(jnp.int32)


def draw_block_lists(key, part):
    stride = QBLOCKS // WINDOW
    own_block = jnp.arange(QBLOCKS, dtype=jnp.int32)[:, None]
    steps_apart = jnp.arange(WINDOW, dtype=jnp.int32)[None, :] * stride
    jitter = jax.random.randint(key, (QBLOCKS, WINDOW), 1, stride)
    offsets = jnp.where(steps_apart == 0, 0, steps_apart + jitter)
    return ((own_block + offsets) % QBLOCKS).astype(jnp.int32)


def draw_block_counts(key, part):
    counts = jax.random.randint(key, (QBLOCKS,), 1, WINDOW + 1)
    return counts.at[0].set(WINDOW).astype(jnp.int32)


def draw_qk_gain(key, part):
    key_dims, key_heads = jax.random.split(key)
    per_dim = jax.random.uniform(key_dims, (2, HEADS, D // HEADS), jnp.float32, 0.7, 1.4)
    per_head = jnp.exp(jax.random.uniform(key_heads, (2, HEADS, 1), jnp.float32, -0.5, 0.7))
    return (per_dim * per_head).reshape(2, D).astype(jnp.float32)


def shard_levels(own_key, extent, shards, low, largest):
    loudness, own = 1.0, jax.random.fold_in(own_key, 6)
    for dim, parts in shards:
        steps = jnp.exp(jax.random.uniform(jax.random.fold_in(own, dim), (parts,), jnp.float32, low / len(shards), largest / len(shards)))
        loudness = loudness * jnp.repeat(steps, extent[dim] // parts).reshape([-1 if axis == dim else 1 for axis in range(len(extent))])
    return loudness


def normal_values(key, extent, spread, reach, cuts=(), kind=jnp.bfloat16):
    drawn = spread * jax.random.normal(key, extent, jnp.float32)
    if cuts:
        drawn = drawn * shard_levels(key, extent, cuts, -0.22, 0.18)
    return jnp.clip(drawn, -reach, reach).astype(kind)


def setup_inputs(seed: int = 0) -> dict:
    key_list = jax.random.split(jax.random.key(seed), 10)
    return {
        "sr_tokens": normal_values(key_list[0], (SEQ_TOK, D), 1.0, 6.0, ((0, 32),)),
        "base_latent": normal_values(key_list[1], (BASE_TOK, D), 1.0, 6.0, ((0, 32),)),
        "upsample_map": draw_upsample_map(jax.random.fold_in(key_list[9], 71), 0),
        "norm_gain": jnp.clip(1.0 + 0.18 * jax.random.normal(key_list[3], (D,), jnp.float32), 0.1, 1.9),
        "w_qkv": normal_values(key_list[4], (3, D, D), D ** -0.5, 0.125, ((2, 4),)),
        "qk_gain": draw_qk_gain(jax.random.fold_in(key_list[9], 71), 0),
        "w_out": normal_values(key_list[6], (D, D), (D // 16) ** -0.5, 0.5, ((0, 4),)),
        "block_lists": draw_block_lists(jax.random.fold_in(key_list[9], 71), 0),
        "block_counts": draw_block_counts(jax.random.fold_in(key_list[9], 71), 0),
    }


EPSILON = 1e-06

def rms_scale(tensor):
    return lax.rsqrt(lax.optimization_barrier(jnp.mean(tensor * tensor, axis=-1, keepdims=True)) + EPSILON)

def block_attend(query_blocks, key_rows, value_rows, block_lists, block_counts):
    head_dim = key_rows.shape[-1]
    key_blocks = key_rows.reshape(-1, BLOCK, head_dim)[block_lists]
    value_blocks = value_rows.reshape(-1, BLOCK, head_dim)[block_lists]
    scores = jnp.einsum('qbd,qwkd->qbwk', query_blocks.astype(jnp.float32), key_blocks.astype(jnp.float32)) * head_dim ** (-0.5)
    allowed = jnp.arange(block_lists.shape[1], dtype=jnp.int32)[None, :] < block_counts[:, None]
    scores = jnp.where(allowed[:, None, :, None], scores, -jnp.inf)
    row_top = lax.optimization_barrier(jnp.max(scores, axis=(2, 3), keepdims=True))
    weights = jnp.exp(scores - row_top)
    row_total = lax.optimization_barrier(jnp.sum(weights, axis=(2, 3)))
    prob_rows = weights.astype(jnp.bfloat16)
    summed = jnp.einsum('qbwk,qwkd->qbd', prob_rows.astype(jnp.float32), value_blocks.astype(jnp.float32))
    return (summed / row_total[:, :, None]).astype(jnp.bfloat16)

def reference(sr_tokens, base_latent, upsample_map, norm_gain, w_qkv, qk_gain, w_out, block_lists, block_counts):
    condition = base_latent[upsample_map]
    mixed_rows = sr_tokens.astype(jnp.float32) + condition.astype(jnp.float32)
    normed = (mixed_rows * rms_scale(mixed_rows) * norm_gain).astype(jnp.bfloat16)
    seq_len = normed.shape[0]
    raw_q = jnp.dot(normed, w_qkv[0], preferred_element_type=jnp.float32).reshape(seq_len, HEADS, HD)
    raw_k = jnp.dot(normed, w_qkv[1], preferred_element_type=jnp.float32).reshape(seq_len, HEADS, HD)
    raw_v = jnp.dot(normed, w_qkv[2], preferred_element_type=jnp.float32).reshape(seq_len, HEADS, HD)
    query_heads = (raw_q * rms_scale(raw_q) * qk_gain[0].reshape(HEADS, HD)).astype(jnp.bfloat16)
    key_heads = (raw_k * rms_scale(raw_k) * qk_gain[1].reshape(HEADS, HD)).astype(jnp.bfloat16)
    value_heads = raw_v.astype(jnp.bfloat16)
    query_stack = query_heads.transpose(1, 0, 2).reshape(HEADS, -1, BLOCK, HD)
    key_stack = key_heads.transpose(1, 0, 2)
    value_stack = value_heads.transpose(1, 0, 2)

    def one_head(operands):
        return block_attend(operands[0], operands[1], operands[2], block_lists, block_counts)
    attended = lax.map(one_head, (query_stack, key_stack, value_stack))
    attended = attended.reshape(HEADS, seq_len, HD).transpose(1, 0, 2).reshape(seq_len, HEADS * HD)
    projected = jnp.dot(attended, w_out, preferred_element_type=jnp.float32)
    return (mixed_rows + projected).astype(jnp.bfloat16)
```

```python
import functools

import jax
import jax.numpy as jnp
from jax import lax
from jax.experimental import pallas as pl
from jax.experimental.pallas import tpu as pltpu
from jax.sharding import Mesh
from jax.sharding import PartitionSpec as P

HD = 128
BASE_FT = 64
BLOCK = 64
EPSILON = 1e-06
SIDE = 4
TILE = 256


F32 = jnp.float32
BF16 = jnp.bfloat16


def ring(step):
    return [(i, (i + step) % SIDE) for i in range(SIDE)]


def swap_cores(x):
    return lax.ppermute(x, "core", [(0, 1), (1, 0)])


def head_norm(raw, gain):
    scale = lax.rsqrt(jnp.mean(raw * raw, axis=-1, keepdims=True) + EPSILON)
    return (raw * scale * gain).astype(BF16)


def kv_kernel(where, sr, before, own, after, spots, gain, w_k, w_v, key_gain, *outs):
    kv_outs, normed_out, mixed_out, held = outs[:4], outs[4], outs[5], outs[6]
    step = pl.program_id(0)
    table = jnp.concatenate([before[...], own[...], after[...]], axis=0)
    rows = lax.broadcasted_iota(jnp.int32, (table.shape[0], TILE), 0)
    chosen = (rows == spots[0]).astype(BF16)
    condition = lax.dot_general(
        chosen, table, (((0,), (0,)), ((), ())), preferred_element_type=F32
    )
    mixed = sr[...].astype(F32) + condition

    @pl.when(step == where[1])
    def _():
        mixed_out[...] = mixed

    scale = lax.rsqrt(jnp.mean(mixed * mixed, axis=-1, keepdims=True) + EPSILON)
    normed = (mixed * scale * gain[...]).astype(BF16)
    normed_out[...] = normed
    raw_k = jnp.dot(normed, w_k[0], preferred_element_type=F32)
    raw_v = jnp.dot(normed, w_v[0], preferred_element_type=F32)
    for head in range(SIDE):
        lanes = slice(head * HD, (head + 1) * HD)
        held[head, 0] = head_norm(raw_k[:, lanes], key_gain[0, :, lanes])
        held[head, 1] = raw_v[:, lanes].astype(BF16)
    for k in range(SIDE):
        kv_outs[k][...] = held[lax.rem(where[0] + k, SIDE)]


def keys_and_values(where, sr, before, own, after, spots, gain, w_qkv, qk_gain):
    rows, width = sr.shape
    cols = w_qkv.shape[2]
    steps = rows // TILE
    same = lambda *idx: lambda i, w: idx
    once = pl.Buffered(1)
    spec = pltpu.PrefetchScalarGridSpec(
        num_scalar_prefetch=1,
        grid=(steps,),
        in_specs=[
            pl.BlockSpec((TILE, width), lambda i, w: (i, 0)),
            pl.BlockSpec(before.shape, same(0, 0), pipeline_mode=once),
            pl.BlockSpec(own.shape, same(0, 0), pipeline_mode=once),
            pl.BlockSpec(after.shape, same(0, 0), pipeline_mode=once),
            pl.BlockSpec((1, 1, TILE), lambda i, w: (i, 0, 0)),
            pl.BlockSpec((1, width), same(0, 0)),
            pl.BlockSpec((1, width, cols), same(1, 0, 0), pipeline_mode=once),
            pl.BlockSpec((1, width, cols), same(2, 0, 0), pipeline_mode=once),
            pl.BlockSpec((1, 1, cols), same(1, 0, 0)),
        ],
        out_specs=[pl.BlockSpec((2, TILE, HD), lambda i, w: (0, i, 0))] * SIDE
        + [
            pl.BlockSpec((TILE, width), lambda i, w: (i, 0)),
            pl.BlockSpec((TILE, width), same(0, 0)),
        ],
        scratch_shapes=[pltpu.VMEM((SIDE, 2, TILE, HD), BF16)],
    )
    return pl.pallas_call(
        kv_kernel,
        grid_spec=spec,
        out_shape=[jax.ShapeDtypeStruct((2, rows, HD), BF16)] * SIDE
        + [
            jax.ShapeDtypeStruct((rows, width), BF16),
            jax.ShapeDtypeStruct((TILE, width), F32),
        ],
        compiler_params=pltpu.CompilerParams(vmem_limit_bytes=48 << 20),
        cost_estimate=pl.CostEstimate(
            flops=2 * rows * width * cols * 2, bytes_accessed=16 << 20, transcendentals=0
        ),
        name="keys_values",
    )(where, sr, before, own, after, spots, gain, w_qkv, w_qkv, qk_gain)


def q_kernel(where, normed, w_q, gain, *outs):
    q_outs, held = outs[:SIDE], outs[SIDE]
    raw = jnp.dot(normed[...], w_q[0], preferred_element_type=F32)
    for head in range(SIDE):
        lanes = slice(head * HD, (head + 1) * HD)
        held[head] = head_norm(raw[:, lanes], gain[0, :, lanes])
    for k in range(SIDE):
        q_outs[k][...] = held[lax.rem(where[0] + k, SIDE)]


def queries(where, normed, w_qkv, qk_gain):
    rows, width = normed.shape
    cols = w_qkv.shape[2]
    spec = pltpu.PrefetchScalarGridSpec(
        num_scalar_prefetch=1,
        grid=(rows // TILE,),
        in_specs=[
            pl.BlockSpec((TILE, width), lambda i, w: (i, 0)),
            pl.BlockSpec((1, width, cols), lambda i, w: (0, 0, 0), pipeline_mode=pl.Buffered(1)),
            pl.BlockSpec((1, 1, cols), lambda i, w: (0, 0, 0)),
        ],
        out_specs=[pl.BlockSpec((TILE, HD), lambda i, w: (i, 0))] * SIDE,
        scratch_shapes=[pltpu.VMEM((SIDE, TILE, HD), BF16)],
    )
    return pl.pallas_call(
        q_kernel,
        grid_spec=spec,
        out_shape=[jax.ShapeDtypeStruct((rows, HD), BF16)] * SIDE,
        compiler_params=pltpu.CompilerParams(vmem_limit_bytes=32 << 20),
        cost_estimate=pl.CostEstimate(
            flops=2 * rows * width * cols, bytes_accessed=8 << 20, transcendentals=0
        ),
        name="queries",
    )(where, normed, w_qkv, qk_gain)


def attend_kernel(where, lists, counts, *refs):
    n_q, n_kv = SIDE, 20
    q_in = refs[:n_q]
    kv_in = refs[n_q : n_q + n_kv]
    out, q_buf, kv_buf, sems = refs[n_q + n_kv :]
    rows = q_in[0].shape[0]
    copies = []

    def begin(src, dst):
        copy = pltpu.make_async_copy(src, dst, sems.at[len(copies)])
        copy.start()
        copies.append(copy)

    for k in range(n_q):
        begin(q_in[k], q_buf.at[pl.ds(k * rows, rows)])
    for core in range(2):
        a0, b0, am, bm, ap, bp, a2k, a2v, b2k, b2v = kv_in[10 * core : 10 * core + 10]
        for dz, a, b in ((0, a0, b0), (1, am, bm), (3, ap, bp)):
            first = (core * SIDE + dz) * SIDE * rows
            begin(a, kv_buf.at[:, pl.ds(first, rows)])
            begin(b, kv_buf.at[:, pl.ds(first + rows, 3 * rows)])
        first = (core * SIDE + 2) * SIDE * rows
        begin(a2k, kv_buf.at[0, pl.ds(first, rows)])
        begin(a2v, kv_buf.at[1, pl.ds(first, rows)])
        begin(b2k, kv_buf.at[0, pl.ds(first + rows, 3 * rows)])
        begin(b2v, kv_buf.at[1, pl.ds(first + rows, 3 * rows)])
    for copy in copies:
        copy.wait()

    window = lists.shape[1]
    keys = window * BLOCK
    lane = lax.broadcasted_iota(jnp.int32, (BLOCK, keys), 1)
    blocks = rows // BLOCK
    share = blocks // SIDE
    together = 4

    def one(i):
        query = q_buf[pl.ds(pl.multiple_of(i * BLOCK, BLOCK), BLOCK), :]
        starts = [pl.multiple_of(lists[i, w] * BLOCK, BLOCK) for w in range(window)]
        key = jnp.concatenate([kv_buf[0, pl.ds(s, BLOCK), :] for s in starts], axis=0)
        value = jnp.concatenate([kv_buf[1, pl.ds(s, BLOCK), :] for s in starts], axis=0)
        scores = lax.dot_general(
            query, key, (((1,), (1,)), ((), ())), preferred_element_type=F32
        ) * HD ** (-0.5)
        scores = jnp.where(lane < counts[i] * BLOCK, scores, -jnp.inf)
        weights = jnp.exp(scores - jnp.max(scores, axis=-1, keepdims=True))
        total = jnp.sum(weights, axis=-1, keepdims=True)
        summed = jnp.dot(weights.astype(BF16), value, preferred_element_type=F32)
        source = lax.rem(where[0] + SIDE - i // blocks, SIDE)
        spot = lax.rem(i, blocks)
        place = pl.multiple_of(lax.rem(spot, share) * BLOCK, BLOCK)
        out[spot // share, source, pl.ds(place, BLOCK), :] = (summed / total).astype(BF16)

    def body(step, carry):
        for j in range(together):
            one(step * together + j)
        return carry

    lax.fori_loop(0, n_q * blocks // together, body, 0)


def attend(where, lists, counts, q_pieces, kv_pieces):
    rows = q_pieces[0].shape[0]
    n = len(q_pieces) + len(kv_pieces)
    spec = pltpu.PrefetchScalarGridSpec(
        num_scalar_prefetch=3,
        grid=(1,),
        in_specs=[pl.BlockSpec(memory_space=pl.ANY)] * n,
        out_specs=pl.BlockSpec((SIDE, SIDE, rows // SIDE, HD), lambda *_: (0, 0, 0, 0)),
        scratch_shapes=[
            pltpu.VMEM((SIDE * rows, HD), BF16),
            pltpu.VMEM((2, 2 * SIDE * SIDE * rows, HD), BF16),
            pltpu.SemaphoreType.DMA((n,)),
        ],
    )
    return pl.pallas_call(
        attend_kernel,
        grid_spec=spec,
        out_shape=jax.ShapeDtypeStruct((SIDE, SIDE, rows // SIDE, HD), BF16),
        compiler_params=pltpu.CompilerParams(vmem_limit_bytes=48 << 20),
        cost_estimate=pl.CostEstimate(
            flops=4 * SIDE * rows * 512 * HD, bytes_accessed=20 << 20, transcendentals=2 << 20
        ),
        name="attend",
    )(where, lists, counts, *q_pieces, *kv_pieces)


def project_kernel(where, attended, *refs):
    w_in, mixed, out = refs[:SIDE], refs[SIDE], refs[SIDE + 1]
    total = mixed[...]
    for k in range(SIDE):
        first = lax.rem(where[1] + SIDE - k, SIDE) * SIDE
        lhs = jnp.concatenate([attended[first + j] for j in range(SIDE)], axis=1)
        if k == 0:
            summed = jnp.dot(lhs, w_in[k][...], preferred_element_type=F32)
        else:
            summed = summed + jnp.dot(lhs, w_in[k][...], preferred_element_type=F32)
    out[0] = (total + summed).astype(BF16)


def project(where, attended, w_pieces, mixed):
    heads, rows, _ = attended.shape
    width = mixed.shape[1]
    depth = w_pieces[0].shape[0]
    part = width // SIDE
    spec = pltpu.PrefetchScalarGridSpec(
        num_scalar_prefetch=1,
        grid=(SIDE,),
        in_specs=[pl.BlockSpec(attended.shape, lambda i, w: (0, 0, 0))]
        + [pl.BlockSpec((depth, part), lambda i, w: (0, i))] * SIDE
        + [pl.BlockSpec((rows, part), lambda i, w: (0, i))],
        out_specs=pl.BlockSpec((1, rows, part), lambda i, w: (i, 0, 0)),
    )
    return pl.pallas_call(
        project_kernel,
        grid_spec=spec,
        out_shape=jax.ShapeDtypeStruct((SIDE, rows, part), BF16),
        compiler_params=pltpu.CompilerParams(vmem_limit_bytes=48 << 20),
        cost_estimate=pl.CostEstimate(
            flops=2 * rows * width * width, bytes_accessed=12 << 20, transcendentals=0
        ),
        name="project",
    )(where, attended, *w_pieces, mixed)


def on_device(
    sr_tokens, base_latent, upsample_map, norm_gain, w_qkv, qk_gain, w_out, block_lists, block_counts
):
    x, y = lax.axis_index("x"), lax.axis_index("y")
    z, core = lax.axis_index("z"), lax.axis_index("core")
    where = jnp.stack([x, y, z, core]).astype(jnp.int32)
    rows = sr_tokens.shape[0]
    seq = ("x", "z", "core")
    count = 2 * SIDE * SIDE
    rank = (x * SIDE + z) * 2 + core

    up = [(i, i + 1) for i in range(count - 1)]
    before = lax.ppermute(base_latent, seq, up)
    after = lax.ppermute(base_latent, seq, [(j, i) for i, j in up])
    spots = (upsample_map - (rank - 1) * BASE_FT).reshape(rows // TILE, 1, TILE)

    w_pieces = [w_out] + [lax.ppermute(w_out, "y", ring(k)) for k in (1, 2, 3)]

    gains = qk_gain.reshape(2, 1, -1)
    *kv, normed, mixed = keys_and_values(
        where, sr_tokens, before, base_latent, after, spots,
        norm_gain.reshape(1, -1), w_qkv, gains,
    )
    q_made = queries(where, normed, w_qkv, gains)

    def gathered(own):
        back = lax.ppermute(own, "z", ring(1))
        ahead = lax.ppermute(own, "z", ring(3))
        far_k = lax.ppermute(back[0], "z", ring(1))
        far_v = lax.ppermute(ahead[1], "z", ring(3))
        return own, back, ahead, far_k, far_v

    near = gathered(kv[0])
    moved = [lax.ppermute(kv[k], "x", ring(k)) for k in (1, 2, 3)]
    q_pieces = [q_made[0]] + [lax.ppermute(q_made[k], "x", ring(k)) for k in (1, 2, 3)]
    others = gathered(jnp.concatenate(moved, axis=1))

    mine = []
    for i in range(3):
        mine += [near[i], others[i]]
    mine += [near[3], near[4], others[3], others[4]]
    kv_pieces = mine + [swap_cores(piece) for piece in mine]

    per = rows // BLOCK
    sources = (lax.rem(x + SIDE - jnp.arange(SIDE, dtype=jnp.int32), SIDE) * SIDE + z) * 2 + core
    lists = block_lists.reshape(count, per, -1)[sources].reshape(SIDE * per, -1)
    counts = block_counts.reshape(count, per)[sources].reshape(-1)
    owner, spot = lists // per, lists % per
    far_core = (owner % 2) ^ core
    far_z = (z + SIDE - (owner // 2) % SIDE) % SIDE
    far_x = (x + SIDE - owner // (2 * SIDE)) % SIDE
    slots = ((far_core * SIDE + far_z) * SIDE + far_x) * per + spot

    attended = attend(where, slots, counts, q_pieces, kv_pieces)
    share = rows // SIDE
    returned = lax.all_to_all(
        attended.reshape(SIDE * SIDE, share, HD), ("y", "x"), split_axis=0, concat_axis=0, tiled=True
    )
    parts = project(where, returned, w_pieces, mixed)
    result = lax.all_to_all(parts, "y", split_axis=0, concat_axis=0, tiled=True)
    return result.reshape(rows, -1)


def solution(mesh):
    chips = Mesh(
        mesh.devices.reshape(SIDE, SIDE, SIDE, 2), ("y", "x", "z", "core")
    )
    seq = ("x", "z", "core")
    placed = (
        P(seq, None),
        P(seq, None),
        P(seq),
        P(),
        P(None, None, "y"),
        P(None, "y"),
        P("y", None),
        P(),
        P(),
    )
    return jax.shard_map(
        on_device, mesh=chips, in_specs=placed, out_specs=P(seq, "y"), check_vma=False
    )
```
